512 devices in a mesh: sec: 64 (over x_hi, z, core), chol: 8 (over y, x_lo).
Axes of the slice: x: 4 (x_hi: 2, x_lo: 2; x = x_hi * 2 + x_lo), y: 4, z: 16, core: 2. Of those that a mesh axis runs over, the one named last changes fastest.
Arguments:
- amplitudes: bfloat16 [64, 16, 1024], P('sec'), may hold values from -3 to 3
- driver: bfloat16 [64, 16, 1024], P('sec'), may hold values from -24 to 24
- x_tiles: bfloat16 [64, 3, 3072, 1024], P('sec', None, 'chol'), may hold values from -0.15625 to 0.15625
- y_tiles: bfloat16 [64, 3, 3072, 1024], P('sec', None, 'chol'), may hold values from -0.15625 to 0.15625
- sources: int32 [64, 3], P('sec'), may hold values from 0 to 63
- live: int32 [64, 3], P('sec'), may hold values from 0 to 1, as said below
- block_tiles: int32 [64, 2], P('sec'), may hold values from 0 to 31
- pairs: int32 [16, 2], replicated, may hold values from 0 to 127
- e_virt: float32 [1024], replicated, may hold values from 0.5 to 3
- e_occ: float32 [128], replicated, may hold values from -2 to -0.3
Outputs:
- updated: bfloat16 [64, 16, 1024], P('sec')
The draws below stay inside these ranges and needn't reach their ends.
Inputs may be any that keep to these rules, and one draw needn't show every extreme that they name: In every tile pair slot 0 is live and live slots come first; some tile pair has all 3 slots live.
All inputs are finite; a program needn't handle non-finite values.
Results may differ from the reference program's by a relative error of at most 0.003.
Values may be sent and summed in bfloat16 or wider, within the bound.
A program may use at most 64 MiB of HBM per device.

```python
import jax
import jax.numpy as jnp
from jax import lax

NV = 1024
NO = 128
NCHOL = 3072
TS = 32
P_SIZE = 16
MCOL = 3
ITERS = 2
NBLK = 64
N_CHOL = 8


def draw_live(key, part):
    first_key, second_key = jax.random.split(jax.random.fold_in(key, 17))
    counts = jax.random.randint(first_key, (NBLK,), 1, MCOL + 1)
    fullest = jax.random.randint(second_key, (), 0, NBLK)
    counts = jnp.where(jnp.arange(NBLK) == fullest, MCOL, counts)
    return (jnp.arange(MCOL)[None, :] < counts[:, None]).astype(jnp.int32)


def with_ends(values, stream_key, smallest, largest):
    shape = values.shape
    index_at = [jax.random.randint(jax.random.fold_in(stream_key, axis), (), 0, shape[axis]) for axis in range(len(shape))]
    values = values.at[tuple(index_at)].set(smallest)
    longest = shape.index(max(shape))
    index_at[longest] = (index_at[longest] + 1) % shape[longest]
    return values.at[tuple(index_at)].set(largest)


def block_levels(key, shape, cuts, low, largest):
    factor_of, own = 1.0, jax.random.fold_in(key, 6)
    for position, parts in cuts:
        heights = jnp.exp(jax.random.uniform(jax.random.fold_in(own, position), (parts,), jnp.float32, low / len(cuts), largest / len(cuts)))
        factor_of = factor_of * jnp.repeat(heights, shape[position] // parts).reshape([-1 if axis == position else 1 for axis in range(len(shape))])
    return factor_of


def centred(stream_key, dims, deviation, reach, cuts=(), kind=jnp.bfloat16):
    values = jax.random.normal(stream_key, dims, jnp.float32) * deviation
    if len(cuts) > 0:
        values = block_levels(stream_key, dims, cuts, -0.22, 0.18) * values
    return jnp.clip(values, min=-reach, max=reach).astype(kind)


def setup_inputs(seed: int = 0) -> dict:
    splits = jax.random.split(jax.random.key(seed), 11)
    amplitudes = centred(splits[0], (NBLK, P_SIZE, TS * TS), 0.5, 3.0, ((0, 64),))
    driver = centred(splits[1], (NBLK, P_SIZE, TS * TS), 4.0, 24.0, ((0, 64),))
    x_tiles = centred(splits[2], (NBLK, MCOL, NCHOL, TS * TS), ((4.0 / (MCOL * TS * TS * NCHOL)) ** 0.25), 0.15625, ((0, 64), (2, 8)))
    y_tiles = centred(splits[3], (NBLK, MCOL, NCHOL, TS * TS), ((4.0 / (MCOL * TS * TS * NCHOL)) ** 0.25), 0.15625, ((0, 64), (2, 8)))
    sources = with_ends(jax.random.randint(splits[4], (NBLK, MCOL), 0, NBLK), jax.random.fold_in(splits[4], 1), 0, NBLK - 1).astype(jnp.int32)
    live = draw_live(jax.random.fold_in(splits[10], 71), 0)
    block_tiles = with_ends(jax.random.randint(splits[6], (NBLK, 2), 0, NV // TS), jax.random.fold_in(splits[6], 1), 0, (NV // TS) - 1).astype(jnp.int32)
    pairs = with_ends(jax.random.randint(splits[7], (P_SIZE, 2), 0, NO), jax.random.fold_in(splits[7], 1), 0, NO - 1).astype(jnp.int32)
    e_virt = jnp.clip(jax.random.uniform(splits[8], (NV,), jnp.float32, 0.5, 3.0), 0.5, 3.0)
    e_occ = jnp.clip(jax.random.uniform(splits[9], (NO,), jnp.float32, -2.0, -0.3), -2.0, -0.3)
    return dict(amplitudes=amplitudes, driver=driver, x_tiles=x_tiles, y_tiles=y_tiles, sources=sources, live=live, block_tiles=block_tiles, pairs=pairs, e_virt=e_virt, e_occ=e_occ)


def integral(left_tile, right_tile):
    product = lax.dot_general(left_tile, right_tile, (((0,), (0,)), ((), ())), preferred_element_type=jnp.float32)
    product = product.reshape(TS, TS, TS, TS).transpose(1, 3, 0, 2)
    return product.reshape(TS * TS, TS * TS).astype(jnp.bfloat16)


def reference(amplitudes, driver, x_tiles, y_tiles, sources, live, block_tiles, pairs, e_virt, e_occ):
    group_size = NCHOL // N_CHOL
    tile_energy = e_virt.reshape(NV // TS, TS)
    energy_a = tile_energy[block_tiles[:, 0]]
    energy_b = tile_energy[block_tiles[:, 1]]
    energy_ij = e_occ[pairs[:, 0]] + e_occ[pairs[:, 1]]
    denominator = (energy_a[:, None, :, None] + energy_b[:, None, None, :] - energy_ij[None, :, None, None]).reshape(NBLK, P_SIZE, TS * TS)
    live_f = live.astype(jnp.float32)
    driven = driver.astype(jnp.float32)
    current = amplitudes
    for sweep in range(ITERS):
        def one_block(operands, current=current):
            left_rows, right_rows, source_ids, live_row = operands
            total = jnp.zeros((P_SIZE, TS * TS), jnp.float32)
            for slot_idx in range(MCOL):
                picked = lax.dynamic_index_in_dim(current, source_ids[slot_idx].astype(jnp.int32), 0, keepdims=False)
                for part_idx in range(N_CHOL):
                    lower = part_idx * group_size
                    built = integral(left_rows[slot_idx, lower:lower + group_size], right_rows[slot_idx, lower:lower + group_size])
                    total = total + live_row[slot_idx] * jnp.dot(picked, built, preferred_element_type=jnp.float32)
            return total

        ladder = lax.map(one_block, (x_tiles, y_tiles, sources, live_f))
        current = (-(driven + ladder) / denominator).astype(jnp.bfloat16)
    return current
```

```python
import jax
import jax.numpy as jnp
from jax import lax
from jax.experimental import pallas as pl
from jax.experimental.pallas import tpu as pltpu
from jax.sharding import PartitionSpec as P

TS = 32
TT = TS * TS
ROWS = 16
SLOTS = 3
DEPTH = 384
NSEC = 64
NCHIP = 32
NCHOL = 8
LANES = 128
MESH = pl.DeviceIdType.MESH
F32 = jnp.float32
BF16 = jnp.bfloat16


def mod(value, size):
    return lax.rem(value + size, size)


def build_column_order(order):
    for part in range(4):
        row = lax.broadcasted_iota(jnp.int32, (256, TT), 0) + part * 256
        col = lax.broadcasted_iota(jnp.int32, (256, TT), 1)
        want = (row & 7) * 128 + ((row >> 3) & 3) * 32 + (row >> 5)
        order[part * 256 : part * 256 + 256, :] = jnp.where(col == want, 1.0, 0.0).astype(BF16)


def build_swap(swap):
    for part in range(4):
        row = lax.broadcasted_iota(jnp.int32, (256, TT), 0) + part * 256
        col = lax.broadcasted_iota(jnp.int32, (256, TT), 1)
        want = (row & 31) * 32 + (row >> 5)
        swap[part * 256 : part * 256 + 256, :] = jnp.where(col == want, 1.0, 0.0).astype(BF16)


def build_integral(slot, xv, yv, order, xp, vs):
    xp[...] = jnp.dot(xv[slot], order[...], preferred_element_type=F32).astype(BF16)

    def chunk(part, carry):
        right = yv[slot, :, pl.ds(pl.multiple_of(part * 256, 256), 256)]
        block = lax.dot_general(
            right, xp[...], (((0,), (0,)), ((), ())), preferred_element_type=F32
        ).astype(BF16)
        for e in range(8):
            for c in range(8):
                column = pl.multiple_of(part * 1024 + e * 128, 128)
                vs[slot, c * 32 : c * 32 + 32, pl.ds(column, 128)] = block[
                    e * 32 : e * 32 + 32, c * 128 : c * 128 + 128
                ]
        return carry

    lax.fori_loop(0, 4, chunk, 0)


def kernel(
    sources, live, tiles, pairs, e_virt, e_occ, amp, drv, x_hbm, y_hbm, out,
    xv, yv, order, swap, xp, vs, left, stack, first, second, picked, part, sums, driven, final,
    load_sem, ag_send, ag_recv, fw_send, fw_recv, pk_send, pk_recv, rs_send, rs_recv,
    fin_send, fin_recv,
):
    sec = lax.axis_index("sec")
    chol = lax.axis_index("chol")
    chip = sec // 2
    core = sec - 2 * chip
    x_hi = chip // 16
    z = chip - 16 * x_hi
    other = 2 * chip + 1 - core
    blocks = (first, second)

    loads = []
    for slot in range(SLOTS):
        pair = (
            pltpu.make_async_copy(x_hbm.at[0, slot], xv.at[slot], load_sem.at[slot]),
            pltpu.make_async_copy(y_hbm.at[0, slot], yv.at[slot], load_sem.at[SLOTS + slot]),
        )
        for copy in pair:
            copy.start()
        loads.append(pair)

    def far_chip(step):
        turn = step // 2
        away = 8 + (1 - 2 * lax.rem(turn, 2)) * ((turn + 1) // 2)
        side = 1 - lax.rem(step, 2)
        return lax.rem(x_hi + side, 2) * 16 + lax.rem(z + away, 16)

    barrier = pltpu.get_barrier_semaphore()

    def greet(step, carry):
        pl.semaphore_signal(
            barrier, inc=1, device_id=(2 * far_chip(step) + core, chol), device_id_type=MESH
        )
        return carry

    lax.fori_loop(0, NCHIP - 1, greet, 0)

    def greet_chol(step, carry):
        pl.semaphore_signal(
            barrier, inc=1, device_id=(sec, lax.rem(chol + step, NCHOL)), device_id_type=MESH
        )
        return carry

    lax.fori_loop(1, NCHOL, greet_chol, 0)
    pl.semaphore_signal(barrier, inc=1, device_id=(other, chol), device_id_type=MESH)

    def gather_copy(turn, step):
        return pltpu.make_async_remote_copy(
            src_ref=blocks[turn].at[sec],
            dst_ref=blocks[turn].at[sec],
            send_sem=ag_send.at[turn, step],
            recv_sem=ag_recv.at[turn, chip],
            device_id=(2 * far_chip(step) + core, chol),
            device_id_type=MESH,
        )

    def gather_arrival(turn, step):
        source = far_chip(step)
        return pltpu.make_async_remote_copy(
            src_ref=blocks[turn].at[sec],
            dst_ref=blocks[turn].at[2 * source + core],
            send_sem=ag_send.at[turn, step],
            recv_sem=ag_recv.at[turn, source],
            device_id=(2 * source + core, chol),
            device_id_type=MESH,
        )

    def forward_copy(turn, source):
        return pltpu.make_async_remote_copy(
            src_ref=blocks[turn].at[2 * source + core],
            dst_ref=blocks[turn].at[2 * source + core],
            send_sem=fw_send.at[turn, source],
            recv_sem=fw_recv.at[turn, source],
            device_id=(other, chol),
            device_id_type=MESH,
        )

    def forward_arrival(turn, source):
        return pltpu.make_async_remote_copy(
            src_ref=blocks[turn].at[2 * source + core],
            dst_ref=blocks[turn].at[2 * source + 1 - core],
            send_sem=fw_send.at[turn, source],
            recv_sem=fw_recv.at[turn, source],
            device_id=(other, chol),
            device_id_type=MESH,
        )

    def gather_start(turn):
        def send(step, carry):
            gather_copy(turn, step).start()
            return carry

        lax.fori_loop(0, NCHIP - 1, send, 0)
        forward_copy(turn, chip).start()

    def gather_finish(turn):
        def take(step, carry):
            back = NCHIP - 2 - step
            gather_arrival(turn, back).wait_recv()
            forward_copy(turn, far_chip(back)).start()
            return carry

        lax.fori_loop(0, NCHIP - 1, take, 0)

        def settle(source, carry):
            forward_arrival(turn, source).wait_recv()
            return carry

        lax.fori_loop(0, NCHIP, settle, 0)

    def gather_drain(turn):
        def drain(step, carry):
            gather_copy(turn, step).wait_send()
            return carry

        lax.fori_loop(0, NCHIP - 1, drain, 0)

        def drain_forward(source, carry):
            forward_copy(turn, source).wait_send()
            return carry

        lax.fori_loop(0, NCHIP, drain_forward, 0)

    def pick_copy(turn, slot_from, peer):
        return pltpu.make_async_remote_copy(
            src_ref=picked.at[turn, chol],
            dst_ref=picked.at[turn, slot_from],
            send_sem=pk_send.at[turn, peer],
            recv_sem=pk_recv.at[turn, slot_from],
            device_id=(sec, peer),
            device_id_type=MESH,
        )

    def share_picks(turn):
        for slot in range(SLOTS):
            chosen = blocks[turn][sources[0, slot]].astype(F32)
            picked[turn, chol, slot] = (chosen * live[0, slot].astype(F32)).astype(BF16)

        def send(step, carry):
            pick_copy(turn, chol, lax.rem(chol + step, NCHOL)).start()
            return carry

        lax.fori_loop(1, NCHOL, send, 0)

        def take(step, carry):
            peer = lax.rem(chol + step, NCHOL)
            pick_copy(turn, peer, peer).wait_recv()
            return carry

        lax.fori_loop(1, NCHOL, take, 0)

    def drain_picks(turn):
        def drain(step, carry):
            pick_copy(turn, chol, lax.rem(chol + step, NCHOL)).wait_send()
            return carry

        lax.fori_loop(1, NCHOL, drain, 0)

    def sum_copy(turn, slot_from, peer):
        return pltpu.make_async_remote_copy(
            src_ref=part.at[turn, peer],
            dst_ref=sums.at[turn, slot_from],
            send_sem=rs_send.at[turn, peer],
            recv_sem=rs_recv.at[turn, slot_from],
            device_id=(sec, peer),
            device_id_type=MESH,
        )

    group = lax.broadcasted_iota(jnp.int32, (ROWS, LANES), 1) >> 5

    def ladder(turn):
        for j in range(NCHOL):
            total = jnp.zeros((4 * ROWS, 4 * LANES), F32)
            for slot in range(SLOTS):
                total += jnp.dot(
                    left[slot], vs[slot, :, j * 512 : j * 512 + 512], preferred_element_type=F32
                )
            joined = None
            for g in range(4):
                block = total[:, g * LANES : g * LANES + LANES]
                own = block[3 * ROWS : 4 * ROWS]
                for w in range(3):
                    own = jnp.where(group == w, block[w * ROWS : w * ROWS + ROWS], own)
                own = own + pltpu.roll(own, 64, 1)
                own = own + pltpu.roll(own, 32, 1)
                joined = own if g == 0 else jnp.where(group == g, own, joined)
            part[turn, j] = joined

    def reduce(turn):
        def send(step, carry):
            sum_copy(turn, chol, lax.rem(chol + step, NCHOL)).start()
            return carry

        lax.fori_loop(1, NCHOL, send, 0)
        sums[turn, chol] = part[turn, chol]

        def take(step, carry):
            peer = lax.rem(chol + step, NCHOL)
            sum_copy(turn, peer, peer).wait_recv()
            return carry

        lax.fori_loop(1, NCHOL, take, 0)
        total = sums[turn, 0]
        for j in range(1, NCHOL):
            total = total + sums[turn, j]
        return total

    def drain_sums(turn):
        def drain(step, carry):
            sum_copy(turn, chol, lax.rem(chol + step, NCHOL)).wait_send()
            return carry

        lax.fori_loop(1, NCHOL, drain, 0)

    def final_copy(slot_from, peer):
        return pltpu.make_async_remote_copy(
            src_ref=final.at[chol],
            dst_ref=final.at[slot_from],
            send_sem=fin_send.at[peer],
            recv_sem=fin_recv.at[slot_from],
            device_id=(sec, peer),
            device_id_type=MESH,
        )

    build_column_order(order)
    for copy in loads[0]:
        copy.wait()
    build_integral(0, xv, yv, order, xp, vs)

    first[sec] = amp[0, :, pl.ds(pl.multiple_of(chol * LANES, LANES), LANES)]
    pl.semaphore_wait(barrier, NCHIP - 1 + NCHOL - 1 + 1)
    gather_start(0)

    for slot in range(1, SLOTS):
        for copy in loads[slot]:
            copy.wait()
        build_integral(slot, xv, yv, order, xp, vs)

    build_swap(swap)
    turned = jnp.dot(drv[0], swap[...], preferred_element_type=F32)
    for j in range(NCHOL):
        driven[j] = turned[:, j * LANES : j * LANES + LANES]
    lane = lax.broadcasted_iota(jnp.int32, (1, LANES), 1)
    energy_a = jnp.zeros((1, LANES), F32)
    for a in range(TS):
        energy_a = jnp.where((lane & 31) == a, e_virt[TS * tiles[0, 0] + a], energy_a)
    energy_b = jnp.zeros((1, LANES), F32)
    for e in range(4):
        energy_b = jnp.where((lane >> 5) == e, e_virt[TS * tiles[0, 1] + 4 * chol + e], energy_b)
    row = lax.broadcasted_iota(jnp.int32, (ROWS, LANES), 0)
    energy_ij = jnp.zeros((ROWS, LANES), F32)
    for p in range(ROWS):
        energy_ij = jnp.where(row == p, e_occ[pairs[0, p]] + e_occ[pairs[1, p]], energy_ij)
    denominator = (energy_a + energy_b) - energy_ij
    own_driven = driven[chol]

    gather_finish(0)
    share_picks(0)
    for slot in range(SLOTS):
        for j in range(NCHOL):
            w, h = j // 2, j % 2
            left[slot, w * ROWS : w * ROWS + ROWS, h * LANES : h * LANES + LANES] = picked[0, j, slot]
    ladder(0)
    second[sec] = (-(own_driven + reduce(0)) / denominator).astype(BF16)
    gather_start(1)
    gather_finish(1)
    share_picks(1)
    for slot in range(SLOTS):
        for j in range(NCHOL):
            stack[slot * ROWS : slot * ROWS + ROWS, j * LANES : j * LANES + LANES] = picked[1, j, slot]
    turned = jnp.dot(stack[...], swap[...], preferred_element_type=F32).astype(BF16)
    for slot in range(SLOTS):
        for w in range(4):
            left[slot, w * ROWS : w * ROWS + ROWS, :] = turned[
                slot * ROWS : slot * ROWS + ROWS, w * 256 : w * 256 + 256
            ]
    ladder(1)
    final[chol] = (-(own_driven + reduce(1)) / denominator).astype(BF16)

    def send_final(step, carry):
        final_copy(chol, lax.rem(chol + step, NCHOL)).start()
        return carry

    lax.fori_loop(1, NCHOL, send_final, 0)

    def take_final(step, carry):
        peer = lax.rem(chol + step, NCHOL)
        final_copy(peer, peer).wait_recv()
        return carry

    lax.fori_loop(1, NCHOL, take_final, 0)
    for j in range(NCHOL):
        stack[0:ROWS, j * LANES : j * LANES + LANES] = final[j]
    out[0] = jnp.dot(stack[0:ROWS, :], swap[...], preferred_element_type=F32).astype(BF16)

    for turn in range(2):
        gather_drain(turn)
        drain_picks(turn)
        drain_sums(turn)

    def drain_final(step, carry):
        final_copy(chol, lax.rem(chol + step, NCHOL)).wait_send()
        return carry

    lax.fori_loop(1, NCHOL, drain_final, 0)


def shards(amplitudes, driver, x_tiles, y_tiles, sources, live, block_tiles, pairs, e_virt, e_occ):
    smem = pl.BlockSpec(memory_space=pltpu.SMEM)
    vmem = pl.BlockSpec(memory_space=pltpu.VMEM)
    hbm = pl.BlockSpec(memory_space=pl.ANY)
    dma = pltpu.SemaphoreType.DMA
    return pl.pallas_call(
        kernel,
        out_shape=jax.ShapeDtypeStruct((1, ROWS, TT), BF16),
        in_specs=[smem] * 6 + [vmem, vmem, hbm, hbm],
        out_specs=vmem,
        scratch_shapes=[
            pltpu.VMEM((SLOTS, DEPTH, TT), BF16),
            pltpu.VMEM((SLOTS, DEPTH, TT), BF16),
            pltpu.VMEM((TT, TT), BF16),
            pltpu.VMEM((TT, TT), BF16),
            pltpu.VMEM((DEPTH, TT), BF16),
            pltpu.VMEM((SLOTS, 256, 4096), BF16),
            pltpu.VMEM((SLOTS, 4 * ROWS, 256), BF16),
            pltpu.VMEM((SLOTS * ROWS, TT), BF16),
            pltpu.VMEM((NSEC, ROWS, LANES), BF16),
            pltpu.VMEM((NSEC, ROWS, LANES), BF16),
            pltpu.VMEM((2, NCHOL, SLOTS, ROWS, LANES), BF16),
            pltpu.VMEM((2, NCHOL, ROWS, LANES), F32),
            pltpu.VMEM((2, NCHOL, ROWS, LANES), F32),
            pltpu.VMEM((NCHOL, ROWS, LANES), F32),
            pltpu.VMEM((NCHOL, ROWS, LANES), BF16),
            dma((2 * SLOTS,)),
            dma((2, NCHIP)),
            dma((2, NCHIP)),
            dma((2, NCHIP)),
            dma((2, NCHIP)),
            dma((2, NCHOL)),
            dma((2, NCHOL)),
            dma((2, NCHOL)),
            dma((2, NCHOL)),
            dma((NCHOL,)),
            dma((NCHOL,)),
        ],
        compiler_params=pltpu.CompilerParams(
            collective_id=0, has_side_effects=True, vmem_limit_bytes=67043328
        ),
        name="ladder_sweeps",
    )(sources, live, block_tiles, pairs.T, e_virt, e_occ, amplitudes, driver, x_tiles, y_tiles)


def solution(mesh):
    placed = (
        P("sec", None, None),
        P("sec", None, None),
        P("sec", None, "chol", None),
        P("sec", None, "chol", None),
        P("sec", None),
        P("sec", None),
        P("sec", None),
        P(),
        P(),
        P(),
    )
    return jax.shard_map(
        shards, mesh=mesh, in_specs=placed, out_specs=P("sec", None, None), check_vma=False
    )
```

```python
import jax
import jax.numpy as jnp
from jax import lax
from jax.experimental import pallas as pl
from jax.experimental.pallas import tpu as pltpu
from jax.sharding import PartitionSpec as P

TS = 32
TT = TS * TS
ROWS = 16
SLOTS = 3
DEPTH = 384
NCHIP = 32
NPAIR = 16
NCHOL = 8
LANES = 128
MESH = pl.DeviceIdType.MESH
F32 = jnp.float32
BF16 = jnp.bfloat16


def build_column_order(order):
    for part in range(4):
        row = lax.broadcasted_iota(jnp.int32, (256, TT), 0) + part * 256
        col = lax.broadcasted_iota(jnp.int32, (256, TT), 1)
        want = (row & 7) * 128 + ((row >> 3) & 3) * 32 + (row >> 5)
        order[part * 256 : part * 256 + 256, :] = jnp.where(col == want, 1.0, 0.0).astype(BF16)


def build_swap(swap):
    for part in range(4):
        row = lax.broadcasted_iota(jnp.int32, (256, TT), 0) + part * 256
        col = lax.broadcasted_iota(jnp.int32, (256, TT), 1)
        want = (row & 31) * 32 + (row >> 5)
        swap[part * 256 : part * 256 + 256, :] = jnp.where(col == want, 1.0, 0.0).astype(BF16)


def build_integral(slot, xv, yv, order, xp, vs):
    xp[...] = jnp.dot(xv[slot], order[...], preferred_element_type=F32).astype(BF16)

    def chunk(part, carry):
        right = yv[slot, :, pl.ds(pl.multiple_of(part * 256, 256), 256)]
        block = lax.dot_general(
            right, xp[...], (((0,), (0,)), ((), ())), preferred_element_type=F32
        ).astype(BF16)
        for e in range(8):
            for c in range(8):
                column = pl.multiple_of(part * 1024 + e * 128, 128)
                vs[slot, c * 32 : c * 32 + 32, pl.ds(column, 128)] = block[
                    e * 32 : e * 32 + 32, c * 128 : c * 128 + 128
                ]
        return carry

    lax.fori_loop(0, 4, chunk, 0)


def kernel(
    sources_hbm, live_hbm, tiles_hbm, pairs_hbm, e_virt_hbm, e_occ_hbm, amp_hbm, drv_hbm, x_hbm,
    y_hbm, out,
    sources, live, tiles, pairs, e_virt, e_occ, amp, drv, xv, yv, order, swap, xp, vs, left, stack, wishes, blocks, offers, picked, part, sums,
    driven, denominator, final,
    small_sem, load_sem, wish_send, wish_recv, ag_send, ag_recv, pk_send, pk_recv, rs_send, rs_recv,
    fin_send, fin_recv,
):
    sec = lax.axis_index("sec")
    chol = lax.axis_index("chol")
    chip = sec // 2
    core = sec - 2 * chip
    x_hi = chip // 16
    z = chip - 16 * x_hi
    other = 2 * chip + 1 - core

    def far_chip(step):
        turn = step // 2
        away = 8 + (1 - 2 * lax.rem(turn, 2)) * ((turn + 1) // 2)
        side = 1 - lax.rem(step, 2)
        return lax.rem(x_hi + side, 2) * 16 + lax.rem(z + away, 16)

    def near_core(step):
        return lax.rem(core + lax.rem(step, 2), 2)

    def near_chol(step):
        return lax.rem(chol + step // 2, NCHOL)

    def near(step):
        return (2 * chip + near_core(step), near_chol(step))

    barrier = pltpu.get_barrier_semaphore()

    def greet(step, carry):
        pl.semaphore_signal(
            barrier, inc=1, device_id=(2 * far_chip(step) + core, chol), device_id_type=MESH
        )
        return carry

    lax.fori_loop(0, NCHIP - 1, greet, 0)

    def greet_near(step, carry):
        pl.semaphore_signal(barrier, inc=1, device_id=near(step), device_id_type=MESH)
        return carry

    lax.fori_loop(1, NPAIR, greet_near, 0)

    small = [
        pltpu.make_async_copy(source, target, small_sem.at[place])
        for place, (source, target) in enumerate(
            (
                (amp_hbm, amp),
                (sources_hbm, sources),
                (live_hbm, live),
                (drv_hbm, drv),
                (tiles_hbm, tiles),
                (pairs_hbm, pairs),
                (e_virt_hbm, e_virt),
                (e_occ_hbm, e_occ),
            )
        )
    ]
    for copy in small:
        copy.start()
    loads = []
    for slot in range(SLOTS):
        pair = (
            pltpu.make_async_copy(x_hbm.at[0, slot], xv.at[slot], load_sem.at[slot]),
            pltpu.make_async_copy(y_hbm.at[0, slot], yv.at[slot], load_sem.at[SLOTS + slot]),
        )
        for copy in pair:
            copy.start()
        loads.append(pair)

    def wish_copy(half):
        return pltpu.make_async_remote_copy(
            src_ref=wishes.at[core],
            dst_ref=wishes.at[half],
            send_sem=wish_send,
            recv_sem=wish_recv,
            device_id=(other, chol),
            device_id_type=MESH,
        )

    def gather_copy(turn, slot_from, step):
        return pltpu.make_async_remote_copy(
            src_ref=blocks.at[turn, chip],
            dst_ref=blocks.at[turn, slot_from],
            send_sem=ag_send.at[turn, step],
            recv_sem=ag_recv.at[turn, slot_from],
            device_id=(2 * far_chip(step) + core, chol),
            device_id_type=MESH,
        )

    def gather_start(turn):
        def send(step, carry):
            gather_copy(turn, chip, step).start()
            return carry

        lax.fori_loop(0, NCHIP - 1, send, 0)

    def pick_copy(turn, half, column, step):
        return pltpu.make_async_remote_copy(
            src_ref=offers.at[turn, near_core(step)],
            dst_ref=picked.at[turn, half, column],
            send_sem=pk_send.at[turn, step],
            recv_sem=pk_recv.at[turn, half, column],
            device_id=near(step),
            device_id_type=MESH,
        )

    def share_picks(turn):
        def take_block(step, carry):
            gather_copy(turn, far_chip(step), step).wait_recv()
            return carry

        lax.fori_loop(0, NCHIP - 1, take_block, 0)
        asked = [
            jnp.broadcast_to(wishes[half, slot : slot + 1, :], (ROWS, LANES))
            for half in range(2)
            for slot in range(SLOTS)
        ]

        def look(source, found):
            block = blocks[turn, source].astype(F32)
            name = (2 * source + core).astype(F32)
            return tuple(jnp.where(a == name, block, f) for a, f in zip(asked, found))

        found = lax.fori_loop(0, NCHIP, look, (jnp.zeros((ROWS, LANES), F32),) * (2 * SLOTS))
        for half in range(2):
            for slot in range(SLOTS):
                offers[turn, half, slot] = found[SLOTS * half + slot].astype(BF16)

        def send(step, carry):
            pick_copy(turn, core, chol, step).start()
            return carry

        lax.fori_loop(1, NPAIR, send, 0)
        picked[turn, core, chol] = offers[turn, core]

        def take(step, carry):
            pick_copy(turn, near_core(step), near_chol(step), step).wait_recv()
            return carry

        lax.fori_loop(1, NPAIR, take, 0)

    def share_drain(turn):
        def drain_block(step, carry):
            gather_copy(turn, chip, step).wait_send()
            return carry

        lax.fori_loop(0, NCHIP - 1, drain_block, 0)

        def drain(step, carry):
            pick_copy(turn, core, chol, step).wait_send()
            return carry

        lax.fori_loop(1, NPAIR, drain, 0)

    def arrived(turn, j, slot):
        return picked[turn, 0, j, slot] + picked[turn, 1, j, slot]

    def sum_copy(slot_from, peer):
        return pltpu.make_async_remote_copy(
            src_ref=part.at[peer],
            dst_ref=sums.at[slot_from],
            send_sem=rs_send.at[peer],
            recv_sem=rs_recv.at[slot_from],
            device_id=(sec, peer),
            device_id_type=MESH,
        )

    def final_copy(half, slot_from, peer):
        return pltpu.make_async_remote_copy(
            src_ref=final.at[half, chol],
            dst_ref=final.at[half, slot_from],
            send_sem=fin_send.at[half, peer],
            recv_sem=fin_recv.at[half, slot_from],
            device_id=(sec, peer),
            device_id_type=MESH,
        )

    group = lax.broadcasted_iota(jnp.int32, (ROWS, LANES), 1) >> 5

    def ladder(j):
        total = jnp.zeros((4 * ROWS, 4 * LANES), F32)
        for slot in range(SLOTS):
            columns = vs[slot, :, pl.ds(pl.multiple_of(j * 512, 512), 512)]
            total += jnp.dot(left[slot], columns, preferred_element_type=F32)
        joined = None
        for g in range(4):
            block = total[:, g * LANES : g * LANES + LANES]
            own = block[3 * ROWS : 4 * ROWS]
            for w in range(3):
                own = jnp.where(group == w, block[w * ROWS : w * ROWS + ROWS], own)
            own = own + pltpu.roll(own, 64, 1)
            own = own + pltpu.roll(own, 32, 1)
            joined = own if g == 0 else jnp.where(group == g, own, joined)
        return joined

    build_column_order(order)
    for copy in small:
        copy.wait()
    for copy in loads[0]:
        copy.wait()
    build_integral(0, xv, yv, order, xp, vs)

    blocks[0, chip] = amp[0, :, pl.ds(pl.multiple_of(chol * LANES, LANES), LANES)]
    asking = jnp.full((8, LANES), -1.0, F32)
    ask_row = lax.broadcasted_iota(jnp.int32, (8, LANES), 0)
    for slot in range(SLOTS):
        wish = (sources[0, slot] + 1) * live[0, slot] - 1
        asking = jnp.where(ask_row == slot, wish.astype(F32), asking)
    wishes[core] = asking
    pl.semaphore_wait(barrier, NCHIP - 1 + NPAIR - 1)
    gather_start(0)

    wish_copy(core).start()

    for slot in range(1, SLOTS):
        for copy in loads[slot]:
            copy.wait()
        build_integral(slot, xv, yv, order, xp, vs)

    build_swap(swap)
    turned = jnp.dot(drv[0], swap[...], preferred_element_type=F32)
    for j in range(NCHOL):
        driven[j] = turned[:, j * LANES : j * LANES + LANES]
    lane = lax.broadcasted_iota(jnp.int32, (1, LANES), 1)
    energy_a = jnp.zeros((1, LANES), F32)
    for a in range(TS):
        energy_a = jnp.where((lane & 31) == a, e_virt[TS * tiles[0, 0] + a], energy_a)
    row = lax.broadcasted_iota(jnp.int32, (ROWS, LANES), 0)
    energy_ij = jnp.zeros((ROWS, LANES), F32)
    for p in range(ROWS):
        energy_ij = jnp.where(row == p, e_occ[pairs[0, p]] + e_occ[pairs[1, p]], energy_ij)
    for j in range(NCHOL):
        energy_b = jnp.zeros((1, LANES), F32)
        for e in range(4):
            energy_b = jnp.where((lane >> 5) == e, e_virt[TS * tiles[0, 1] + 4 * j + e], energy_b)
        denominator[j] = (energy_a + energy_b) - energy_ij

    wish_copy(1 - core).wait_recv()
    share_picks(0)
    for slot in range(SLOTS):
        for j in range(NCHOL):
            w, h = j // 2, j % 2
            left[slot, w * ROWS : w * ROWS + ROWS, h * LANES : h * LANES + LANES] = arrived(0, j, slot)
    for step in range(1, NCHOL + 1):
        j = lax.rem(chol + step, NCHOL)
        if step < NCHOL:
            part[j] = ladder(j)
            sum_copy(chol, j).start()
        else:
            sums[chol] = ladder(j)

    def take_sum(step, carry):
        peer = lax.rem(chol + step, NCHOL)
        sum_copy(peer, peer).wait_recv()
        return carry

    lax.fori_loop(1, NCHOL, take_sum, 0)
    total = driven[chol]
    for j in range(NCHOL):
        total = total + sums[j]
    blocks[1, chip] = (-total / denominator[chol]).astype(BF16)
    gather_start(1)
    share_picks(1)
    for slot in range(SLOTS):
        for j in range(NCHOL):
            stack[slot * ROWS : slot * ROWS + ROWS, j * LANES : j * LANES + LANES] = arrived(1, j, slot)
    turned = jnp.dot(stack[...], swap[...], preferred_element_type=F32).astype(BF16)
    for slot in range(SLOTS):
        for w in range(4):
            left[slot, w * ROWS : w * ROWS + ROWS, :] = turned[
                slot * ROWS : slot * ROWS + ROWS, w * 256 : w * 256 + 256
            ]
    for half in range(2):
        for j in range(4):
            final[half, chol, j] = ladder(4 * half + j).astype(BF16)

        def send_final(step, carry, half=half):
            final_copy(half, chol, lax.rem(chol + step, NCHOL)).start()
            return carry

        lax.fori_loop(1, NCHOL, send_final, 0)
    for half in range(2):

        def take_final(step, carry, half=half):
            peer = lax.rem(chol + step, NCHOL)
            final_copy(half, peer, peer).wait_recv()
            return carry

        lax.fori_loop(1, NCHOL, take_final, 0)
        for j in range(4):
            total = driven[4 * half + j]
            for source in range(NCHOL):
                total = total + final[half, source, j].astype(F32)
            at = (4 * half + j) * LANES
            stack[0:ROWS, at : at + LANES] = (-total / denominator[4 * half + j]).astype(BF16)
    out[0] = jnp.dot(stack[0:ROWS, :], swap[...], preferred_element_type=F32).astype(BF16)

    wish_copy(core).wait_send()
    share_drain(0)
    share_drain(1)

    def drain_sums(step, carry):
        peer = lax.rem(chol + step, NCHOL)
        sum_copy(chol, peer).wait_send()
        for half in range(2):
            final_copy(half, chol, peer).wait_send()
        return carry

    lax.fori_loop(1, NCHOL, drain_sums, 0)


def shards(amplitudes, driver, x_tiles, y_tiles, sources, live, block_tiles, pairs, e_virt, e_occ):
    vmem = pl.BlockSpec(memory_space=pltpu.VMEM)
    hbm = pl.BlockSpec(memory_space=pl.ANY)
    dma = pltpu.SemaphoreType.DMA
    return pl.pallas_call(
        kernel,
        out_shape=jax.ShapeDtypeStruct((1, ROWS, TT), BF16),
        in_specs=[hbm] * 10,
        out_specs=vmem,
        scratch_shapes=[
            pltpu.SMEM((1, SLOTS), jnp.int32),
            pltpu.SMEM((1, SLOTS), jnp.int32),
            pltpu.SMEM((1, 2), jnp.int32),
            pltpu.SMEM((2, ROWS), jnp.int32),
            pltpu.SMEM((TT,), F32),
            pltpu.SMEM((LANES,), F32),
            pltpu.VMEM((1, ROWS, TT), BF16),
            pltpu.VMEM((1, ROWS, TT), BF16),
            pltpu.VMEM((SLOTS, DEPTH, TT), BF16),
            pltpu.VMEM((SLOTS, DEPTH, TT), BF16),
            pltpu.VMEM((TT, TT), BF16),
            pltpu.VMEM((TT, TT), BF16),
            pltpu.VMEM((DEPTH, TT), BF16),
            pltpu.VMEM((SLOTS, 256, 4096), BF16),
            pltpu.VMEM((SLOTS, 4 * ROWS, 256), BF16),
            pltpu.VMEM((SLOTS * ROWS, TT), BF16),
            pltpu.VMEM((2, 8, LANES), F32),
            pltpu.VMEM((2, NCHIP, ROWS, LANES), BF16),
            pltpu.VMEM((2, 2, SLOTS, ROWS, LANES), BF16),
            pltpu.VMEM((2, 2, NCHOL, SLOTS, ROWS, LANES), BF16),
            pltpu.VMEM((NCHOL, ROWS, LANES), F32),
            pltpu.VMEM((NCHOL, ROWS, LANES), F32),
            pltpu.VMEM((NCHOL, ROWS, LANES), F32),
            pltpu.VMEM((NCHOL, ROWS, LANES), F32),
            pltpu.VMEM((2, NCHOL, 4, ROWS, LANES), BF16),
            dma((8,)),
            dma((2 * SLOTS,)),
            dma,
            dma,
            dma((2, NCHIP)),
            dma((2, NCHIP)),
            dma((2, NPAIR)),
            dma((2, 2, NCHOL)),
            dma((NCHOL,)),
            dma((NCHOL,)),
            dma((2, NCHOL)),
            dma((2, NCHOL)),
        ],
        compiler_params=pltpu.CompilerParams(
            collective_id=0, has_side_effects=True, vmem_limit_bytes=67043328
        ),
        name="ladder_sweeps",
    )(sources, live, block_tiles, pairs.T, e_virt, e_occ, amplitudes, driver, x_tiles, y_tiles)


def solution(mesh):
    placed = (
        P("sec", None, None),
        P("sec", None, None),
        P("sec", None, "chol", None),
        P("sec", None, "chol", None),
        P("sec", None),
        P("sec", None),
        P("sec", None),
        P(),
        P(),
        P(),
    )
    return jax.shard_map(
        shards, mesh=mesh, in_specs=placed, out_specs=P("sec", None, None), check_vma=False
    )
```

```python
import jax
import jax.numpy as jnp
from jax import lax
from jax.experimental import pallas as pl
from jax.experimental.pallas import tpu as pltpu
from jax.sharding import PartitionSpec as P

TS = 32
TT = TS * TS
ROWS = 16
SLOTS = 3
DEPTH = 384
NCHIP = 32
NPAIR = 16
NCHOL = 8
LANES = 128
MESH = pl.DeviceIdType.MESH
F32 = jnp.float32
BF16 = jnp.bfloat16


def build_column_order(order):
    for part in range(4):
        row = lax.broadcasted_iota(jnp.int32, (256, TT), 0) + part * 256
        col = lax.broadcasted_iota(jnp.int32, (256, TT), 1)
        want = (row & 7) * 128 + ((row >> 3) & 3) * 32 + (row >> 5)
        order[part * 256 : part * 256 + 256, :] = jnp.where(col == want, 1.0, 0.0).astype(BF16)


def build_swap(swap):
    for part in range(4):
        row = lax.broadcasted_iota(jnp.int32, (256, TT), 0) + part * 256
        col = lax.broadcasted_iota(jnp.int32, (256, TT), 1)
        want = (row & 31) * 32 + (row >> 5)
        swap[part * 256 : part * 256 + 256, :] = jnp.where(col == want, 1.0, 0.0).astype(BF16)


def build_integral(slot, xv, yv, order, xp, vs):
    xp[...] = jnp.dot(xv[slot], order[...], preferred_element_type=F32).astype(BF16)

    def chunk(part, carry):
        right = yv[slot, :, pl.ds(pl.multiple_of(part * 256, 256), 256)]
        block = lax.dot_general(
            right, xp[...], (((0,), (0,)), ((), ())), preferred_element_type=F32
        ).astype(BF16)
        for e in range(8):
            for c in range(8):
                column = pl.multiple_of(part * 1024 + e * 128, 128)
                vs[slot, c * 32 : c * 32 + 32, pl.ds(column, 128)] = block[
                    e * 32 : e * 32 + 32, c * 128 : c * 128 + 128
                ]
        return carry

    lax.fori_loop(0, 4, chunk, 0)


def kernel(
    sources_hbm, live_hbm, tiles_hbm, pairs_hbm, e_virt_hbm, e_occ_hbm, amp_hbm, drv_hbm, x_hbm,
    y_hbm, out,
    sources, live, tiles, pairs, e_virt, e_occ, amp, drv, xv, yv, order, swap, xp, vs, left, stack, wishes, blocks, offers, picked, part, sums,
    driven, denominator, final,
    small_sem, load_sem, wish_send, wish_recv, ag_send, ag_recv, pk_send, pk_recv, rs_send, rs_recv,
    fin_send, fin_recv,
):
    sec = lax.axis_index("sec")
    chol = lax.axis_index("chol")
    chip = sec // 2
    core = sec - 2 * chip
    x_hi = chip // 16
    z = chip - 16 * x_hi
    other = 2 * chip + 1 - core

    def far_chip(step):
        turn = step // 2
        away = 8 + (1 - 2 * lax.rem(turn, 2)) * ((turn + 1) // 2)
        side = 1 - lax.rem(step, 2)
        return lax.rem(x_hi + side, 2) * 16 + lax.rem(z + away, 16)

    def near_core(step):
        return lax.rem(core + lax.rem(step, 2), 2)

    def near_chol(step):
        return lax.rem(chol + step // 2, NCHOL)

    def near(step):
        return (2 * chip + near_core(step), near_chol(step))

    barrier = pltpu.get_barrier_semaphore()

    def greet(step, carry):
        pl.semaphore_signal(
            barrier, inc=1, device_id=(2 * far_chip(step) + core, chol), device_id_type=MESH
        )
        return carry

    lax.fori_loop(0, NCHIP - 1, greet, 0)

    def greet_near(step, carry):
        pl.semaphore_signal(barrier, inc=1, device_id=near(step), device_id_type=MESH)
        return carry

    lax.fori_loop(1, NPAIR, greet_near, 0)

    small = [
        pltpu.make_async_copy(source, target, small_sem.at[place])
        for place, (source, target) in enumerate(
            (
                (amp_hbm, amp),
                (sources_hbm, sources),
                (live_hbm, live),
                (drv_hbm, drv),
                (tiles_hbm, tiles),
                (pairs_hbm, pairs),
                (e_virt_hbm, e_virt),
                (e_occ_hbm, e_occ),
            )
        )
    ]
    for copy in small:
        copy.start()
    loads = []
    for slot in range(SLOTS):
        pair = (
            pltpu.make_async_copy(x_hbm.at[0, slot], xv.at[slot], load_sem.at[slot]),
            pltpu.make_async_copy(y_hbm.at[0, slot], yv.at[slot], load_sem.at[SLOTS + slot]),
        )
        for copy in pair:
            copy.start()
        loads.append(pair)

    def wish_copy(half):
        return pltpu.make_async_remote_copy(
            src_ref=wishes.at[core],
            dst_ref=wishes.at[half],
            send_sem=wish_send,
            recv_sem=wish_recv,
            device_id=(other, chol),
            device_id_type=MESH,
        )

    def gather_copy(turn, slot_from, step):
        return pltpu.make_async_remote_copy(
            src_ref=blocks.at[turn, chip],
            dst_ref=blocks.at[turn, slot_from],
            send_sem=ag_send.at[turn, step],
            recv_sem=ag_recv.at[turn, slot_from],
            device_id=(2 * far_chip(step) + core, chol),
            device_id_type=MESH,
        )

    def gather_start(turn):
        def send(step, carry):
            gather_copy(turn, chip, step).start()
            return carry

        lax.fori_loop(0, NCHIP - 1, send, 0)

    def pick_copy(turn, half, column, step):
        return pltpu.make_async_remote_copy(
            src_ref=offers.at[turn, near_core(step)],
            dst_ref=picked.at[turn, half, column],
            send_sem=pk_send.at[turn, step],
            recv_sem=pk_recv.at[turn, half, column],
            device_id=near(step),
            device_id_type=MESH,
        )

    def share_picks(turn):
        asked = [
            jnp.broadcast_to(wishes[half, slot : slot + 1, :], (ROWS, LANES))
            for half in range(2)
            for slot in range(SLOTS)
        ]

        def look(source, found):
            block = blocks[turn, source].astype(F32)
            name = (2 * source + core).astype(F32)
            return tuple(jnp.where(a == name, block, f) for a, f in zip(asked, found))

        def take_block(step, found):
            back = NCHIP - 2 - step
            source = far_chip(back)
            gather_copy(turn, source, back).wait_recv()
            return look(source, found)

        found = look(chip, (jnp.zeros((ROWS, LANES), F32),) * (2 * SLOTS))
        found = lax.fori_loop(0, NCHIP - 1, take_block, found)
        for half in range(2):
            for slot in range(SLOTS):
                offers[turn, half, slot] = found[SLOTS * half + slot].astype(BF16)

        def send(step, carry):
            pick_copy(turn, core, chol, step).start()
            return carry

        lax.fori_loop(1, NPAIR, send, 0)
        picked[turn, core, chol] = offers[turn, core]

        def take(step, carry):
            pick_copy(turn, near_core(step), near_chol(step), step).wait_recv()
            return carry

        lax.fori_loop(1, NPAIR, take, 0)

    def share_drain(turn):
        def drain_block(step, carry):
            gather_copy(turn, chip, step).wait_send()
            return carry

        lax.fori_loop(0, NCHIP - 1, drain_block, 0)

        def drain(step, carry):
            pick_copy(turn, core, chol, step).wait_send()
            return carry

        lax.fori_loop(1, NPAIR, drain, 0)

    def arrived(turn, j, slot):
        return picked[turn, 0, j, slot] + picked[turn, 1, j, slot]

    def sum_copy(slot_from, peer):
        return pltpu.make_async_remote_copy(
            src_ref=part.at[peer],
            dst_ref=sums.at[slot_from],
            send_sem=rs_send.at[peer],
            recv_sem=rs_recv.at[slot_from],
            device_id=(sec, peer),
            device_id_type=MESH,
        )

    def final_copy(half, slot_from, peer):
        return pltpu.make_async_remote_copy(
            src_ref=final.at[half, chol],
            dst_ref=final.at[half, slot_from],
            send_sem=fin_send.at[half, peer],
            recv_sem=fin_recv.at[half, slot_from],
            device_id=(sec, peer),
            device_id_type=MESH,
        )

    group = lax.broadcasted_iota(jnp.int32, (ROWS, LANES), 1) >> 5

    def ladder(j):
        total = jnp.zeros((4 * ROWS, 4 * LANES), F32)
        for slot in range(SLOTS):
            columns = vs[slot, :, pl.ds(pl.multiple_of(j * 512, 512), 512)]
            total += jnp.dot(left[slot], columns, preferred_element_type=F32)
        joined = None
        for g in range(4):
            block = total[:, g * LANES : g * LANES + LANES]
            own = block[3 * ROWS : 4 * ROWS]
            for w in range(3):
                own = jnp.where(group == w, block[w * ROWS : w * ROWS + ROWS], own)
            own = own + pltpu.roll(own, 64, 1)
            own = own + pltpu.roll(own, 32, 1)
            joined = own if g == 0 else jnp.where(group == g, own, joined)
        return joined

    build_column_order(order)
    for copy in small:
        copy.wait()
    for copy in loads[0]:
        copy.wait()
    build_integral(0, xv, yv, order, xp, vs)

    blocks[0, chip] = amp[0, :, pl.ds(pl.multiple_of(chol * LANES, LANES), LANES)]
    asking = jnp.full((8, LANES), -1.0, F32)
    ask_row = lax.broadcasted_iota(jnp.int32, (8, LANES), 0)
    for slot in range(SLOTS):
        wish = (sources[0, slot] + 1) * live[0, slot] - 1
        asking = jnp.where(ask_row == slot, wish.astype(F32), asking)
    wishes[core] = asking
    pl.semaphore_wait(barrier, NCHIP - 1 + NPAIR - 1)
    gather_start(0)

    wish_copy(core).start()

    for slot in range(1, SLOTS):
        for copy in loads[slot]:
            copy.wait()
        build_integral(slot, xv, yv, order, xp, vs)

    build_swap(swap)
    turned = jnp.dot(drv[0], swap[...], preferred_element_type=F32)
    for j in range(NCHOL):
        driven[j] = turned[:, j * LANES : j * LANES + LANES]
    lane = lax.broadcasted_iota(jnp.int32, (1, LANES), 1)
    energy_a = jnp.zeros((1, LANES), F32)
    for a in range(TS):
        energy_a = jnp.where((lane & 31) == a, e_virt[TS * tiles[0, 0] + a], energy_a)
    row = lax.broadcasted_iota(jnp.int32, (ROWS, LANES), 0)
    energy_ij = jnp.zeros((ROWS, LANES), F32)
    for p in range(ROWS):
        energy_ij = jnp.where(row == p, e_occ[pairs[0, p]] + e_occ[pairs[1, p]], energy_ij)
    for j in range(NCHOL):
        energy_b = jnp.zeros((1, LANES), F32)
        for e in range(4):
            energy_b = jnp.where((lane >> 5) == e, e_virt[TS * tiles[0, 1] + 4 * j + e], energy_b)
        denominator[j] = (energy_a + energy_b) - energy_ij

    wish_copy(1 - core).wait_recv()
    share_picks(0)
    for slot in range(SLOTS):
        for j in range(NCHOL):
            w, h = j // 2, j % 2
            left[slot, w * ROWS : w * ROWS + ROWS, h * LANES : h * LANES + LANES] = arrived(0, j, slot)
    for step in range(1, NCHOL + 1):
        j = lax.rem(chol + step, NCHOL)
        if step < NCHOL:
            part[j] = ladder(j)
            sum_copy(chol, j).start()
        else:
            sums[chol] = ladder(j)

    def take_sum(step, carry):
        peer = lax.rem(chol + step, NCHOL)
        sum_copy(peer, peer).wait_recv()
        return carry

    lax.fori_loop(1, NCHOL, take_sum, 0)
    total = driven[chol]
    for j in range(NCHOL):
        total = total + sums[j]
    blocks[1, chip] = (-total / denominator[chol]).astype(BF16)
    gather_start(1)
    wish_copy(core).wait_send()
    share_drain(0)
    share_picks(1)
    for slot in range(SLOTS):
        for j in range(NCHOL):
            stack[slot * ROWS : slot * ROWS + ROWS, j * LANES : j * LANES + LANES] = arrived(1, j, slot)
    turned = jnp.dot(stack[...], swap[...], preferred_element_type=F32).astype(BF16)
    for slot in range(SLOTS):
        for w in range(4):
            left[slot, w * ROWS : w * ROWS + ROWS, :] = turned[
                slot * ROWS : slot * ROWS + ROWS, w * 256 : w * 256 + 256
            ]
    for half in range(2):
        for j in range(4):
            final[half, chol, j] = ladder(4 * half + j).astype(BF16)

        def send_final(step, carry, half=half):
            final_copy(half, chol, lax.rem(chol + step, NCHOL)).start()
            return carry

        lax.fori_loop(1, NCHOL, send_final, 0)
    share_drain(1)

    def drain_sums(step, carry):
        sum_copy(chol, lax.rem(chol + step, NCHOL)).wait_send()
        return carry

    lax.fori_loop(1, NCHOL, drain_sums, 0)
    for half in range(2):

        def take_final(step, carry, half=half):
            peer = lax.rem(chol + step, NCHOL)
            final_copy(half, peer, peer).wait_recv()
            return carry

        lax.fori_loop(1, NCHOL, take_final, 0)
        for j in range(4):
            total = driven[4 * half + j]
            for source in range(NCHOL):
                total = total + final[half, source, j].astype(F32)
            at = (4 * half + j) * LANES
            stack[0:ROWS, at : at + LANES] = (-total / denominator[4 * half + j]).astype(BF16)
    out[0] = jnp.dot(stack[0:ROWS, :], swap[...], preferred_element_type=F32).astype(BF16)

    def drain_final(step, carry):
        for half in range(2):
            final_copy(half, chol, lax.rem(chol + step, NCHOL)).wait_send()
        return carry

    lax.fori_loop(1, NCHOL, drain_final, 0)


def shards(amplitudes, driver, x_tiles, y_tiles, sources, live, block_tiles, pairs, e_virt, e_occ):
    vmem = pl.BlockSpec(memory_space=pltpu.VMEM)
    hbm = pl.BlockSpec(memory_space=pltpu.HBM)
    dma = pltpu.SemaphoreType.DMA
    operands = (
        sources, live, block_tiles, pairs.T, e_virt, e_occ, amplitudes, driver, x_tiles, y_tiles,
    )
    return pl.pallas_call(
        kernel,
        out_shape=jax.ShapeDtypeStruct((1, ROWS, TT), BF16),
        in_specs=[hbm] * 10,
        out_specs=vmem,
        scratch_shapes=[
            pltpu.SMEM((1, SLOTS), jnp.int32),
            pltpu.SMEM((1, SLOTS), jnp.int32),
            pltpu.SMEM((1, 2), jnp.int32),
            pltpu.SMEM((2, ROWS), jnp.int32),
            pltpu.SMEM((TT,), F32),
            pltpu.SMEM((LANES,), F32),
            pltpu.VMEM((1, ROWS, TT), BF16),
            pltpu.VMEM((1, ROWS, TT), BF16),
            pltpu.VMEM((SLOTS, DEPTH, TT), BF16),
            pltpu.VMEM((SLOTS, DEPTH, TT), BF16),
            pltpu.VMEM((TT, TT), BF16),
            pltpu.VMEM((TT, TT), BF16),
            pltpu.VMEM((DEPTH, TT), BF16),
            pltpu.VMEM((SLOTS, 256, 4096), BF16),
            pltpu.VMEM((SLOTS, 4 * ROWS, 256), BF16),
            pltpu.VMEM((SLOTS * ROWS, TT), BF16),
            pltpu.VMEM((2, 8, LANES), F32),
            pltpu.VMEM((2, NCHIP, ROWS, LANES), BF16),
            pltpu.VMEM((2, 2, SLOTS, ROWS, LANES), BF16),
            pltpu.VMEM((2, 2, NCHOL, SLOTS, ROWS, LANES), BF16),
            pltpu.VMEM((NCHOL, ROWS, LANES), F32),
            pltpu.VMEM((NCHOL, ROWS, LANES), F32),
            pltpu.VMEM((NCHOL, ROWS, LANES), F32),
            pltpu.VMEM((NCHOL, ROWS, LANES), F32),
            pltpu.VMEM((2, NCHOL, 4, ROWS, LANES), BF16),
            dma((8,)),
            dma((2 * SLOTS,)),
            dma,
            dma,
            dma((2, NCHIP)),
            dma((2, NCHIP)),
            dma((2, NPAIR)),
            dma((2, 2, NCHOL)),
            dma((NCHOL,)),
            dma((NCHOL,)),
            dma((2, NCHOL)),
            dma((2, NCHOL)),
        ],
        compiler_params=pltpu.CompilerParams(
            collective_id=0, has_side_effects=True, vmem_limit_bytes=48 * 1024 * 1024
        ),
        name="ladder_sweeps",
    )(*(pltpu.with_memory_space_constraint(operand, pltpu.HBM) for operand in operands))


def solution(mesh):
    placed = (
        P("sec", None, None),
        P("sec", None, None),
        P("sec", None, "chol", None),
        P("sec", None, "chol", None),
        P("sec", None),
        P("sec", None),
        P("sec", None),
        P(),
        P(),
        P(),
    )
    return jax.shard_map(
        shards, mesh=mesh, in_specs=placed, out_specs=P("sec", None, None), check_vma=False
    )
```

```python
import jax
import jax.numpy as jnp
from jax import lax
from jax.experimental import pallas as pl
from jax.experimental.pallas import tpu as pltpu
from jax.sharding import PartitionSpec as P

TS = 32
TT = TS * TS
ROWS = 16
SLOTS = 3
DEPTH = 384
NCHIP = 32
NPAIR = 16
NCHOL = 8
LANES = 128
MESH = pl.DeviceIdType.MESH
F32 = jnp.float32
BF16 = jnp.bfloat16


def rem(value, size):
    return value % size if isinstance(value, int) else lax.rem(value, size)


def build_column_order(order):
    for part in range(4):
        row = lax.broadcasted_iota(jnp.int32, (256, TT), 0) + part * 256
        col = lax.broadcasted_iota(jnp.int32, (256, TT), 1)
        want = (row & 7) * 128 + ((row >> 3) & 3) * 32 + (row >> 5)
        order[part * 256 : part * 256 + 256, :] = jnp.where(col == want, 1.0, 0.0).astype(BF16)


def build_swap(swap):
    for part in range(4):
        row = lax.broadcasted_iota(jnp.int32, (256, TT), 0) + part * 256
        col = lax.broadcasted_iota(jnp.int32, (256, TT), 1)
        want = (row & 31) * 32 + (row >> 5)
        swap[part * 256 : part * 256 + 256, :] = jnp.where(col == want, 1.0, 0.0).astype(BF16)


def build_integral(slot, xv, yv, order, xp, vs):
    xp[...] = jnp.dot(xv[slot], order[...], preferred_element_type=F32).astype(BF16)

    def chunk(part, carry):
        right = yv[slot, :, pl.ds(pl.multiple_of(part * 256, 256), 256)]
        block = lax.dot_general(
            right, xp[...], (((0,), (0,)), ((), ())), preferred_element_type=F32
        ).astype(BF16)
        for e in range(8):
            for c in range(8):
                column = pl.multiple_of(part * 1024 + e * 128, 128)
                vs[slot, c * 32 : c * 32 + 32, pl.ds(column, 128)] = block[
                    e * 32 : e * 32 + 32, c * 128 : c * 128 + 128
                ]
        return carry

    lax.fori_loop(0, 4, chunk, 0)


def kernel(
    sources_hbm, live_hbm, tiles_hbm, pairs_hbm, e_virt_hbm, e_occ_hbm, amp_hbm, drv_hbm, x_hbm,
    y_hbm, out,
    sources, live, tiles, pairs, e_virt, e_occ, amp, drv, xv, yv, order, swap, xp, vs, left, stack, wishes, blocks, offers, picked, part, sums,
    driven, denominator, final,
    small_sem, load_sem, wish_send, wish_recv, ag_send, ag_recv, pk_send, pk_recv, rs_send, rs_recv,
    fin_send, fin_recv,
):
    sec = lax.axis_index("sec")
    chol = lax.axis_index("chol")
    chip = sec // 2
    core = sec - 2 * chip
    x_hi = chip // 16
    z = chip - 16 * x_hi
    other = 2 * chip + 1 - core

    def far_chip(step):
        turn = step // 2
        away = 8 + (1 - 2 * rem(turn, 2)) * ((turn + 1) // 2)
        side = 1 - rem(step, 2)
        return lax.rem(x_hi + side, 2) * 16 + lax.rem(z + away, 16)

    def near_core(step):
        return lax.rem(core + rem(step, 2), 2)

    def near_chol(step):
        return lax.rem(chol + step // 2, NCHOL)

    def near(step):
        return (2 * chip + near_core(step), near_chol(step))

    barrier = pltpu.get_barrier_semaphore()

    def greet(step, carry):
        pl.semaphore_signal(
            barrier, inc=1, device_id=(2 * far_chip(step) + core, chol), device_id_type=MESH
        )
        return carry

    for step in range(NCHIP - 1):
        greet(step, 0)

    def greet_near(step, carry):
        pl.semaphore_signal(barrier, inc=1, device_id=near(step), device_id_type=MESH)
        return carry

    for step in range(1, NPAIR):
        greet_near(step, 0)

    small = [
        pltpu.make_async_copy(source, target, small_sem.at[place])
        for place, (source, target) in enumerate(
            (
                (amp_hbm, amp),
                (sources_hbm, sources),
                (live_hbm, live),
                (drv_hbm, drv),
                (tiles_hbm, tiles),
                (pairs_hbm, pairs),
                (e_virt_hbm, e_virt),
                (e_occ_hbm, e_occ),
            )
        )
    ]
    for copy in small:
        copy.start()
    loads = []
    for slot in range(SLOTS):
        pair = (
            pltpu.make_async_copy(x_hbm.at[0, slot], xv.at[slot], load_sem.at[slot]),
            pltpu.make_async_copy(y_hbm.at[0, slot], yv.at[slot], load_sem.at[SLOTS + slot]),
        )
        for copy in pair:
            copy.start()
        loads.append(pair)

    def wish_copy(half):
        return pltpu.make_async_remote_copy(
            src_ref=wishes.at[core],
            dst_ref=wishes.at[half],
            send_sem=wish_send,
            recv_sem=wish_recv,
            device_id=(other, chol),
            device_id_type=MESH,
        )

    def gather_copy(turn, slot_from, step):
        return pltpu.make_async_remote_copy(
            src_ref=blocks.at[turn, chip],
            dst_ref=blocks.at[turn, slot_from],
            send_sem=ag_send.at[turn, step],
            recv_sem=ag_recv.at[turn, slot_from],
            device_id=(2 * far_chip(step) + core, chol),
            device_id_type=MESH,
        )

    def gather_start(turn):
        for step in range(NCHIP - 1):
            gather_copy(turn, chip, step).start()

    def pick_copy(turn, half, column, step):
        return pltpu.make_async_remote_copy(
            src_ref=offers.at[turn, near_core(step)],
            dst_ref=picked.at[turn, half, column],
            send_sem=pk_send.at[turn, step],
            recv_sem=pk_recv.at[turn, half, column],
            device_id=near(step),
            device_id_type=MESH,
        )

    def share_picks(turn):
        asked = [
            jnp.broadcast_to(wishes[half, slot : slot + 1, :], (ROWS, LANES))
            for half in range(2)
            for slot in range(SLOTS)
        ]

        def look(source, found):
            block = blocks[turn, source].astype(F32)
            name = (2 * source + core).astype(F32)
            return tuple(jnp.where(a == name, block, f) for a, f in zip(asked, found))

        def take_block(step, found):
            back = NCHIP - 2 - step
            source = far_chip(back)
            gather_copy(turn, source, back).wait_recv()
            return look(source, found)

        found = look(chip, (jnp.zeros((ROWS, LANES), F32),) * (2 * SLOTS))
        found = lax.fori_loop(0, NCHIP - 1, take_block, found)
        for half in range(2):
            for slot in range(SLOTS):
                offers[turn, half, slot] = found[SLOTS * half + slot].astype(BF16)

        for step in range(1, NPAIR):
            pick_copy(turn, core, chol, step).start()
        picked[turn, core, chol] = offers[turn, core]

        def take(step, carry):
            pick_copy(turn, near_core(step), near_chol(step), step).wait_recv()
            return carry

        lax.fori_loop(1, NPAIR, take, 0)

    def share_drain(turn):
        def drain_block(step, carry):
            gather_copy(turn, chip, step).wait_send()
            return carry

        lax.fori_loop(0, NCHIP - 1, drain_block, 0)

        def drain(step, carry):
            pick_copy(turn, core, chol, step).wait_send()
            return carry

        lax.fori_loop(1, NPAIR, drain, 0)

    def arrived(turn, j, slot):
        return picked[turn, 0, j, slot] + picked[turn, 1, j, slot]

    def sum_copy(slot_from, peer):
        return pltpu.make_async_remote_copy(
            src_ref=part.at[peer],
            dst_ref=sums.at[slot_from],
            send_sem=rs_send.at[peer],
            recv_sem=rs_recv.at[slot_from],
            device_id=(sec, peer),
            device_id_type=MESH,
        )

    def final_copy(half, slot_from, peer):
        return pltpu.make_async_remote_copy(
            src_ref=final.at[half, chol],
            dst_ref=final.at[half, slot_from],
            send_sem=fin_send.at[half, peer],
            recv_sem=fin_recv.at[half, slot_from],
            device_id=(sec, peer),
            device_id_type=MESH,
        )

    group = lax.broadcasted_iota(jnp.int32, (ROWS, LANES), 1) >> 5

    def ladder(j):
        total = jnp.zeros((4 * ROWS, 4 * LANES), F32)
        for slot in range(SLOTS):
            columns = vs[slot, :, pl.ds(pl.multiple_of(j * 512, 512), 512)]
            total += jnp.dot(left[slot], columns, preferred_element_type=F32)
        joined = None
        for g in range(4):
            block = total[:, g * LANES : g * LANES + LANES]
            own = block[3 * ROWS : 4 * ROWS]
            for w in range(3):
                own = jnp.where(group == w, block[w * ROWS : w * ROWS + ROWS], own)
            own = own + pltpu.roll(own, 64, 1)
            own = own + pltpu.roll(own, 32, 1)
            joined = own if g == 0 else jnp.where(group == g, own, joined)
        return joined

    build_column_order(order)
    for copy in small:
        copy.wait()
    for copy in loads[0]:
        copy.wait()
    build_integral(0, xv, yv, order, xp, vs)

    blocks[0, chip] = amp[0, :, pl.ds(pl.multiple_of(chol * LANES, LANES), LANES)]
    asking = jnp.full((8, LANES), -1.0, F32)
    ask_row = lax.broadcasted_iota(jnp.int32, (8, LANES), 0)
    for slot in range(SLOTS):
        wish = (sources[0, slot] + 1) * live[0, slot] - 1
        asking = jnp.where(ask_row == slot, wish.astype(F32), asking)
    wishes[core] = asking
    pl.semaphore_wait(barrier, NCHIP - 1 + NPAIR - 1)
    gather_start(0)

    wish_copy(core).start()

    for slot in range(1, SLOTS):
        for copy in loads[slot]:
            copy.wait()
        build_integral(slot, xv, yv, order, xp, vs)

    build_swap(swap)
    turned = jnp.dot(drv[0], swap[...], preferred_element_type=F32)
    for j in range(NCHOL):
        driven[j] = turned[:, j * LANES : j * LANES + LANES]
    lane = lax.broadcasted_iota(jnp.int32, (1, LANES), 1)
    energy_a = jnp.zeros((1, LANES), F32)
    for a in range(TS):
        energy_a = jnp.where((lane & 31) == a, e_virt[TS * tiles[0, 0] + a], energy_a)
    row = lax.broadcasted_iota(jnp.int32, (ROWS, LANES), 0)
    energy_ij = jnp.zeros((ROWS, LANES), F32)
    for p in range(ROWS):
        energy_ij = jnp.where(row == p, e_occ[pairs[0, p]] + e_occ[pairs[1, p]], energy_ij)
    for j in range(NCHOL):
        energy_b = jnp.zeros((1, LANES), F32)
        for e in range(4):
            energy_b = jnp.where((lane >> 5) == e, e_virt[TS * tiles[0, 1] + 4 * j + e], energy_b)
        denominator[j] = (energy_a + energy_b) - energy_ij

    wish_copy(1 - core).wait_recv()
    share_picks(0)
    for slot in range(SLOTS):
        for j in range(NCHOL):
            w, h = j // 2, j % 2
            left[slot, w * ROWS : w * ROWS + ROWS, h * LANES : h * LANES + LANES] = arrived(0, j, slot)
    for step in range(1, NCHOL + 1):
        j = lax.rem(chol + step, NCHOL)
        if step < NCHOL:
            part[j] = ladder(j)
            sum_copy(chol, j).start()
        else:
            sums[chol] = ladder(j)

    def take_sum(step, carry):
        peer = lax.rem(chol + step, NCHOL)
        sum_copy(peer, peer).wait_recv()
        return carry

    lax.fori_loop(1, NCHOL, take_sum, 0)
    total = driven[chol]
    for j in range(NCHOL):
        total = total + sums[j]
    blocks[1, chip] = (-total / denominator[chol]).astype(BF16)
    gather_start(1)
    wish_copy(core).wait_send()
    share_drain(0)
    share_picks(1)
    for slot in range(SLOTS):
        for j in range(NCHOL):
            stack[slot * ROWS : slot * ROWS + ROWS, j * LANES : j * LANES + LANES] = arrived(1, j, slot)
    turned = jnp.dot(stack[...], swap[...], preferred_element_type=F32).astype(BF16)
    for slot in range(SLOTS):
        for w in range(4):
            left[slot, w * ROWS : w * ROWS + ROWS, :] = turned[
                slot * ROWS : slot * ROWS + ROWS, w * 256 : w * 256 + 256
            ]
    for half in range(2):
        for j in range(4):
            final[half, chol, j] = ladder(4 * half + j).astype(BF16)

        def send_final(step, carry, half=half):
            final_copy(half, chol, lax.rem(chol + step, NCHOL)).start()
            return carry

        lax.fori_loop(1, NCHOL, send_final, 0)
    share_drain(1)

    def drain_sums(step, carry):
        sum_copy(chol, lax.rem(chol + step, NCHOL)).wait_send()
        return carry

    lax.fori_loop(1, NCHOL, drain_sums, 0)
    for half in range(2):

        def take_final(step, carry, half=half):
            peer = lax.rem(chol + step, NCHOL)
            final_copy(half, peer, peer).wait_recv()
            return carry

        lax.fori_loop(1, NCHOL, take_final, 0)
        for j in range(4):
            total = driven[4 * half + j]
            for source in range(NCHOL):
                total = total + final[half, source, j].astype(F32)
            at = (4 * half + j) * LANES
            stack[0:ROWS, at : at + LANES] = (-total / denominator[4 * half + j]).astype(BF16)
    out[0] = jnp.dot(stack[0:ROWS, :], swap[...], preferred_element_type=F32).astype(BF16)

    def drain_final(step, carry):
        for half in range(2):
            final_copy(half, chol, lax.rem(chol + step, NCHOL)).wait_send()
        return carry

    lax.fori_loop(1, NCHOL, drain_final, 0)


def shards(amplitudes, driver, x_tiles, y_tiles, sources, live, block_tiles, pairs, e_virt, e_occ):
    vmem = pl.BlockSpec(memory_space=pltpu.VMEM)
    hbm = pl.BlockSpec(memory_space=pltpu.HBM)
    dma = pltpu.SemaphoreType.DMA
    operands = (
        sources, live, block_tiles, pairs.T, e_virt, e_occ, amplitudes, driver, x_tiles, y_tiles,
    )
    return pl.pallas_call(
        kernel,
        out_shape=jax.ShapeDtypeStruct((1, ROWS, TT), BF16),
        in_specs=[hbm] * 10,
        out_specs=vmem,
        scratch_shapes=[
            pltpu.SMEM((1, SLOTS), jnp.int32),
            pltpu.SMEM((1, SLOTS), jnp.int32),
            pltpu.SMEM((1, 2), jnp.int32),
            pltpu.SMEM((2, ROWS), jnp.int32),
            pltpu.SMEM((TT,), F32),
            pltpu.SMEM((LANES,), F32),
            pltpu.VMEM((1, ROWS, TT), BF16),
            pltpu.VMEM((1, ROWS, TT), BF16),
            pltpu.VMEM((SLOTS, DEPTH, TT), BF16),
            pltpu.VMEM((SLOTS, DEPTH, TT), BF16),
            pltpu.VMEM((TT, TT), BF16),
            pltpu.VMEM((TT, TT), BF16),
            pltpu.VMEM((DEPTH, TT), BF16),
            pltpu.VMEM((SLOTS, 256, 4096), BF16),
            pltpu.VMEM((SLOTS, 4 * ROWS, 256), BF16),
            pltpu.VMEM((SLOTS * ROWS, TT), BF16),
            pltpu.VMEM((2, 8, LANES), F32),
            pltpu.VMEM((2, NCHIP, ROWS, LANES), BF16),
            pltpu.VMEM((2, 2, SLOTS, ROWS, LANES), BF16),
            pltpu.VMEM((2, 2, NCHOL, SLOTS, ROWS, LANES), BF16),
            pltpu.VMEM((NCHOL, ROWS, LANES), F32),
            pltpu.VMEM((NCHOL, ROWS, LANES), F32),
            pltpu.VMEM((NCHOL, ROWS, LANES), F32),
            pltpu.VMEM((NCHOL, ROWS, LANES), F32),
            pltpu.VMEM((2, NCHOL, 4, ROWS, LANES), BF16),
            dma((8,)),
            dma((2 * SLOTS,)),
            dma,
            dma,
            dma((2, NCHIP)),
            dma((2, NCHIP)),
            dma((2, NPAIR)),
            dma((2, 2, NCHOL)),
            dma((NCHOL,)),
            dma((NCHOL,)),
            dma((2, NCHOL)),
            dma((2, NCHOL)),
        ],
        compiler_params=pltpu.CompilerParams(
            collective_id=0, has_side_effects=True, vmem_limit_bytes=48 * 1024 * 1024
        ),
        name="ladder_sweeps",
    )(*(pltpu.with_memory_space_constraint(operand, pltpu.HBM) for operand in operands))


def solution(mesh):
    placed = (
        P("sec", None, None),
        P("sec", None, None),
        P("sec", None, "chol", None),
        P("sec", None, "chol", None),
        P("sec", None),
        P("sec", None),
        P("sec", None),
        P(),
        P(),
        P(),
    )
    return jax.shard_map(
        shards, mesh=mesh, in_specs=placed, out_specs=P("sec", None, None), check_vma=False
    )
```
